32 devices in a mesh: groups: 2 (over x), width: 16 (over z, y, core).
Axes of the slice: x: 2, y: 2, z: 4, core: 2. Of those that a mesh axis runs over, the one named last changes fastest.
Arguments:
- stream_in: bfloat16 [2, 128, 8192], P(None, 'groups', 'width'), parts along dimension 1, may hold values from -16 to 16
- norm_gain: float32 [2, 8192], replicated, may hold values from 0.1 to 1.9
- w_gate: bfloat16 [2, 8192, 14336], P(None, None, 'width'), may hold values from -0.0625 to 0.0625
- w_up: bfloat16 [2, 8192, 14336], P(None, None, 'width'), may hold values from -0.0625 to 0.0625
- w_down: bfloat16 [2, 14336, 8192], P(None, 'width'), may hold values from -0.0625 to 0.0625
Outputs:
- stream_out: bfloat16 [2, 128, 8192], P(None, 'groups', 'width'), parts along dimension 1
The draws below stay inside these ranges and needn't reach their ends.
There are 2 independent parts, one for each index of `groups`. The reference program is written for one: setup_inputs(seed, part) draws one part's arguments, and reference() takes and returns one part's arrays. A program takes and returns all parts, laid end to end along the dimension named above; an argument that names none is the same for every part. Nothing has to cross between parts.
All inputs are finite; a program needn't handle non-finite values.
Results may differ from the reference program's by a relative error of at most 0.012.
Values may be sent and summed in bfloat16 or wider, within the bound.
A program may use at most 192 MiB of HBM per device.

```python
import math
import jax
import jax.numpy as jnp
from jax import lax

D = 8192
FF = 14336
LAYERS = 2
MICRO = 2
ROWS = 64


def draw_stream_in(key, part):
    key_base, key_column, key_row = jax.random.split(key, 3)
    column_pos = jnp.arange(D, dtype=jnp.float32) / (D - 1)
    column_scale = 3.0 ** column_pos / 3.0 * jnp.exp(jax.random.uniform(key_column, (D,), jnp.float32, math.log(0.55), math.log(1.8)))
    base_values = jax.random.normal(key_base, (MICRO, ROWS, D), jnp.float32)
    row_scale = jnp.exp(jax.random.uniform(key_row, (MICRO, ROWS, 1), jnp.float32, math.log(0.3), math.log(3.0)))
    values = jnp.clip(base_values * row_scale * column_scale, -16.0, 16.0)
    return values.astype(jnp.bfloat16)


def with_spikes(array, key, source, target, parts, factor):
    owner, partner = [(jnp.arange(array.shape[dim]) // (array.shape[dim] // parts)).reshape([-1 if axis == dim else 1 for axis in range(array.ndim)]) for dim in (source, target)]
    chosen = jax.random.permutation(key, parts)[partner]
    strong = (owner == chosen) | (owner == (partner + parts // 2) % parts)
    return jnp.where(strong, factor * array, array)


def level_of(stream_key, extent, shards, smallest, top_value):
    def one(position, blocks):
        draws = jax.random.uniform(jax.random.fold_in(jax.random.fold_in(stream_key, 6), position), (blocks,), jnp.float32, smallest / len(shards), top_value / len(shards))
        return jnp.repeat(jnp.exp(draws), extent[position] // blocks).reshape((-1,) + (1,) * (len(extent) - position - 1))

    factor_of = one(*shards[0])
    for cut in shards[1:]:
        factor_of = factor_of * one(*cut)
    return factor_of


def bell_draw(key, extent, width, limit, cuts=(), kind=jnp.bfloat16):
    drawn = width * jax.random.normal(key, extent, jnp.float32)
    if cuts:
        drawn = drawn * level_of(key, extent, cuts, -0.22, 0.18)
    return jnp.clip(drawn, -limit, limit).astype(kind)


def bell_draw_with(key, shape, deviation, limit, pieces, heavy, kind=jnp.bfloat16):
    values = deviation * jax.random.normal(key, shape, jnp.float32)
    if pieces:
        values = values * level_of(key, shape, pieces, -0.22, 0.18)
    return jnp.clip(with_spikes(values, jax.random.fold_in(key, 3), *heavy), -limit, limit).astype(kind)


def setup_inputs(seed: int = 0, part: int = 0) -> dict:
    seeds = jax.random.split(jax.random.key(seed), 6)
    own_keys = jax.random.split(jax.random.fold_in(seeds[5], part), 6)
    stream_in = draw_stream_in(jax.random.fold_in(jax.random.fold_in(seeds[5], part), 71), part)
    norm_gain = jnp.clip(1.0 + 0.18 * jax.random.normal(seeds[1], (LAYERS, D), jnp.float32), 0.1, 1.9)
    w_gate = bell_draw(seeds[2], (LAYERS, D, FF), D ** -0.5, 0.0625, ((2, 16),))
    w_up = bell_draw(seeds[3], (LAYERS, D, FF), D ** -0.5, 0.0625, ((2, 16),))
    w_down = bell_draw_with(seeds[4], (LAYERS, FF, D), FF ** -0.5, 0.0625, ((1, 16),), (1, 2, 16, 2.0))
    return dict(stream_in=stream_in, norm_gain=norm_gain, w_gate=w_gate, w_up=w_up, w_down=w_down)


def sublayer(stream, gain_row, gate_weight, up_weight, down_weight):
    stream_f = stream.astype(jnp.float32)
    meansq = lax.optimization_barrier(jnp.mean(stream_f * stream_f, axis=1, keepdims=True))
    normed = (stream_f * lax.rsqrt(meansq + 1e-05) * gain_row).astype(jnp.bfloat16)
    gate_out = jnp.dot(normed, gate_weight, preferred_element_type=jnp.float32)
    up_out = jnp.dot(normed, up_weight, preferred_element_type=jnp.float32)
    hidden = (jax.nn.silu(gate_out) * up_out).astype(jnp.bfloat16)
    branch = jnp.dot(hidden, down_weight, preferred_element_type=jnp.float32)
    return (stream_f + branch).astype(jnp.bfloat16)

def reference(stream_in, norm_gain, w_gate, w_up, w_down):
    results = []
    for micro_index in range(MICRO):
        stream = stream_in[micro_index]
        for depth in range(LAYERS):
            stream = sublayer(stream, norm_gain[depth], w_gate[depth], w_up[depth], w_down[depth])
        results.append(stream)
    return jnp.stack(results)
```

```python
import functools

import jax
import jax.numpy as jnp
from jax import lax
from jax.experimental import pallas as pl
from jax.experimental.pallas import tpu as pltpu
from jax.sharding import PartitionSpec as P

MESH = pl.DeviceIdType.MESH


def plain_body(stream_in, norm_gain, w_gate, w_up, w_down):
    micro, rows, own_width = stream_in.shape
    stream = stream_in.reshape(micro * rows, own_width)
    for depth in range(w_gate.shape[0]):
        whole = lax.all_gather(stream, "width", axis=1, tiled=True).astype(jnp.float32)
        meansq = jnp.mean(whole * whole, axis=1, keepdims=True)
        normed = (whole * lax.rsqrt(meansq + 1e-05) * norm_gain[depth]).astype(jnp.bfloat16)
        gate_out = jnp.dot(normed, w_gate[depth], preferred_element_type=jnp.float32)
        up_out = jnp.dot(normed, w_up[depth], preferred_element_type=jnp.float32)
        hidden = (jax.nn.silu(gate_out) * up_out).astype(jnp.bfloat16)
        partials = jnp.dot(hidden, w_down[depth], preferred_element_type=jnp.float32)
        branch = lax.psum_scatter(partials, "width", scatter_dimension=1, tiled=True)
        stream = (stream.astype(jnp.float32) + branch).astype(jnp.bfloat16)
    return stream.reshape(micro, rows, own_width)


SPLIT = 2


def kernel(
    n, x_ref, gain_ref, wg_ref, wu_ref, wd_ref, out_ref,
    pair_w, down_w, parts, scaled, acc, squares, hidden, own,
    core_out, core_in, y_out, y_in, z_out, z_in, keep,
    pair_sem, down_sem, gather_send, gather_recv, sum_send, core_recv, y_recv, z_recv,
):
    layers = wg_ref.shape[0]
    m, width = x_ref.shape
    rows = m // SPLIT
    chips, nz = n // 2, n // 4
    chunk = 2 * width
    me = lax.axis_index("width")
    c, y, z = lax.rem(me, 2), lax.rem(me // 2, 2), me // 4

    def device(zi, yi, ci):
        return (zi * 2 + yi) * 2 + ci

    low = z < nz // 2
    inner = (z == 1) | (z == nz - 2)
    mate = z + 1 - 2 * lax.rem(z, 2)
    cross, beyond = jnp.where(low, nz - 2, 1), jnp.where(low, nz - 1, 0)
    core_peer, y_peer = device(z, y, 1 - c), device(z, 1 - y, c)
    near_order = [z, mate, cross, beyond]
    sum_order = [jnp.where(inner, a, b) for a, b in zip([mate, beyond, cross, z], [beyond, cross, mate, z])]

    def pick(i, values):
        value = values[0]
        for at in range(1, len(values)):
            value = jnp.where(i == at, values[at], value)
        return value

    def pair_copy(depth, chip, j):
        src = wg_ref if j == 0 else wu_ref
        span = pl.ds(pl.multiple_of(chip * chunk, chunk), chunk)
        return pltpu.make_async_copy(src.at[depth, span, :], pair_w.at[chip, j], pair_sem.at[chip, j])

    def down_copy(depth, chip):
        cols = pl.ds(pl.multiple_of(chip * chunk, chunk), chunk)
        return pltpu.make_async_copy(wd_ref.at[depth, :, cols], down_w.at[chip], down_sem.at[chip])

    def remote(src, dst, send, recv, dev):
        return pltpu.make_async_remote_copy(
            src_ref=src, dst_ref=dst, send_sem=send, recv_sem=recv,
            device_id={"width": dev}, device_id_type=MESH,
        )

    def piece(h):
        return pl.ds(h * rows, rows)

    sequence = [near_order[0] * 2 + y, near_order[1] * 2 + y, near_order[0] * 2 + 1 - y]
    sequence += [near_order[k] * 2 + y for k in range(2, nz)] + [near_order[k] * 2 + 1 - y for k in range(1, nz)]
    sums = [zi * 2 + 1 - y for zi in sum_order] + [zi * 2 + y for zi in sum_order]

    def load_pair(chip):
        pair_copy(0, chip, 0).start()
        pair_copy(0, chip, 1).start()

    load_pair(sequence[0])

    barrier = pltpu.get_barrier_semaphore()
    peers = [core_peer, y_peer] + [device(zi, y, c) for zi in near_order[1:]]
    for peer in peers:
        pl.semaphore_signal(barrier, inc=1, device_id={"width": peer}, device_id_type=MESH)

    for chip in sequence[1:]:
        load_pair(chip)

    for chip in sums:
        down_copy(0, chip).start()

    pl.semaphore_wait(barrier, len(peers))

    class Layer:
        def __init__(self, depth):
            self.depth = depth
            self.mine = x_ref if depth == 0 else own.at[depth]

        def to_peer(self, h, owner, dev, mine=False):
            dst = self.part(owner, h)
            src = self.mine.at[piece(h)] if mine else dst
            return remote(src, dst, gather_send.at[self.depth], gather_recv.at[self.depth, h, owner], dev)

        def part(self, owner, h):
            return parts.at[self.depth, owner, piece(h)]

        def arrived(self, h, owner):
            self.to_peer(h, owner, core_peer).wait_recv()

        def send_own(self, h):
            self.to_peer(h, me, device(mate, y, c), True).start()
            self.to_peer(h, me, y_peer, True).start()
            self.to_peer(h, me, device(cross, y, c), True).start()
            self.to_peer(h, me, core_peer, True).start()
            parts[self.depth, me, piece(h)] = self.mine[piece(h)]

        def clear(self):
            acc[...] = jnp.zeros_like(acc)
            squares[...] = jnp.zeros_like(squares)

        def pass_z(self, h, k):
            owner = device(near_order[k], y, c)
            self.arrived(h, owner)
            if k > 1:
                @pl.when(inner)
                def _():
                    self.to_peer(h, owner, device(mate, y, c)).start()
            self.to_peer(h, owner, y_peer).start()
            self.to_peer(h, owner, core_peer).start()

        def pass_y(self, h, k):
            owner = device(near_order[k], 1 - y, c)
            self.arrived(h, owner)
            self.to_peer(h, owner, core_peer).start()

        def gate_up(self, i):
            depth = self.depth
            chip = pick(i, sequence)
            for h in range(SPLIT):
                self.arrived(h, chip * 2 + 1 - c)
            for h in range(2):
                block = parts[depth, chip * 2 + h].astype(jnp.float32)
                cols = pl.ds(pl.multiple_of((chip * 2 + h) * width, width), width)
                scaled[:, h * width:(h + 1) * width] = (block * gain_ref[depth:depth + 1, cols]).astype(jnp.bfloat16)
                sq = block * block
                total = sq[:, :128]
                for j in range(1, width // 128):
                    total = total + sq[:, j * 128:(j + 1) * 128]
                squares[...] += total
            for j in range(2):
                pair_copy(depth, chip, j).wait()
            for j in range(2):
                acc[j] += jnp.dot(scaled[...], pair_w[chip, j], preferred_element_type=jnp.float32)
            if depth + 1 < layers:
                for j in range(2):
                    pair_copy(depth + 1, chip, j).start()

        def make_hidden(self):
            meansq = jnp.sum(squares[...], axis=1, keepdims=True) / (n * width)
            scale = lax.rsqrt(meansq + 1e-05)
            gate_out = acc[0] * scale
            hidden[...] = (gate_out / (1.0 + jnp.exp(-gate_out)) * (acc[1] * scale)).astype(jnp.bfloat16)

        def core_copy(self, chip):
            return remote(core_out.at[self.depth, chip], core_in.at[self.depth, chip],
                          sum_send.at[self.depth], core_recv.at[self.depth, chip], core_peer)

        def y_copy(self, h, zi):
            return remote(y_out.at[self.depth, zi, piece(h)], y_in.at[self.depth, zi, piece(h)],
                          sum_send.at[self.depth], y_recv.at[self.depth, h, zi], y_peer)

        def z_copy(self, h, t, slot, zi):
            return remote(z_out.at[self.depth, t, piece(h)], z_in.at[self.depth, slot, piece(h)],
                          sum_send.at[self.depth], z_recv.at[self.depth, h, slot], device(zi, y, c))

        def down(self, t):
            chip = pick(t, sums)
            down_copy(self.depth, chip).wait()
            both = jnp.dot(hidden[...], down_w[chip], preferred_element_type=jnp.float32)
            left, right = both[:, :width], both[:, width:]
            core_out[self.depth, chip] = jnp.where(c == 0, right, left).astype(jnp.bfloat16)
            self.core_copy(chip).start()
            keep[chip] = jnp.where(c == 0, left, right)
            if self.depth + 1 < layers:
                down_copy(self.depth + 1, chip).start()

        def core_sum(self, h, chip):
            return keep[chip, piece(h)] + core_in[self.depth, chip, piece(h)].astype(jnp.float32)

        def far(self, h, t):
            zi, chip = sum_order[t], sums[t]
            if h == 0:
                self.core_copy(chip).wait_recv()
            y_out[self.depth, zi, piece(h)] = self.core_sum(h, chip).astype(jnp.bfloat16)
            self.y_copy(h, zi).start()

        def near_sum(self, h, t):
            zi, chip = sum_order[t], sums[nz + t]
            if h == 0:
                self.core_copy(chip).wait_recv()
            self.y_copy(h, zi).wait_recv()
            return self.core_sum(h, chip) + y_in[self.depth, zi, piece(h)].astype(jnp.float32)

        def near(self, h, t):
            total = self.near_sum(h, t)
            if t == 0:
                z_out[self.depth, t, piece(h)] = total.astype(jnp.bfloat16)
            else:
                @pl.when(inner)
                def _():
                    self.z_copy(h, t, t - 1, mate).wait_recv()
                    met = z_in[self.depth, t - 1, piece(h)].astype(jnp.float32)
                    z_out[self.depth, t, piece(h)] = (total + met).astype(jnp.bfloat16)

                @pl.when(jnp.logical_not(inner))
                def _():
                    z_out[self.depth, t, piece(h)] = total.astype(jnp.bfloat16)
            slot = jnp.where(inner, 2 if t == 0 else 3, t)
            self.z_copy(h, t, slot, jnp.where(inner, sum_order[t], mate)).start()

        def final(self, h):
            total = self.near_sum(h, nz - 1) + self.mine[piece(h)].astype(jnp.float32)
            for slot in (2, 3):
                self.z_copy(h, 0, slot, mate).wait_recv()
                total = total + z_in[self.depth, slot, piece(h)].astype(jnp.float32)
            if self.depth + 1 < layers:
                own[self.depth + 1, piece(h)] = total.astype(jnp.bfloat16)
                Layer(self.depth + 1).send_own(h)
            else:
                out_ref[piece(h)] = total.astype(jnp.bfloat16)

        def sent(self):
            whole = parts.at[self.depth, pl.ds(0, n - 2)]
            pltpu.make_async_copy(whole, whole, gather_send.at[self.depth]).wait()

            @pl.when(inner)
            def _():
                two = parts.at[self.depth, pl.ds(0, nz - 2)]
                pltpu.make_async_copy(two, two, gather_send.at[self.depth]).wait()

            whole = parts.at[self.depth, pl.ds(0, n - 1)]
            pltpu.make_async_copy(whole, whole, sum_send.at[self.depth]).wait()

    def steps(count, tasks, body):
        @pl.loop(0, count)
        def _(i):
            for at in sorted(set(at for at, _ in tasks)):
                @pl.when(i == at)
                def _():
                    for where, task in tasks:
                        if where == at:
                            task()
            body(i)

    def call(method, *args):
        return lambda: method(*args)

    every = [Layer(depth) for depth in range(layers)]
    for depth, layer in enumerate(every):
        if depth == 0:
            for h in range(SPLIT):
                layer.send_own(h)
        layer.clear()
        tasks = []
        H = range(SPLIT)
        tasks += [(1, call(layer.pass_z, h, 1)) for h in H] + [(1, call(layer.pass_y, h, 0)) for h in H]
        tasks += [(k, call(layer.pass_z, h, k)) for k in range(2, nz) for h in H]
        tasks += [(k + 3, call(layer.pass_y, h, k)) for k in range(1, nz) for h in H]
        steps(chips, tasks, layer.gate_up)
        layer.make_hidden()
        tasks = []
        tasks += [(t + 2, call(layer.far, h, t)) for t in range(nz) for h in range(SPLIT)]
        steps(chips, tasks, layer.down)
        before = layer
        for t in range(nz - 1):
            for h in range(SPLIT):
                layer.near(h, t)
        for h in range(SPLIT):
            layer.final(h)
    for layer in every:
        layer.sent()


def fused(n, stream_in, norm_gain, w_gate, w_up, w_down):
    micro, rows, width = stream_in.shape
    layers, d, ff = w_gate.shape
    m, chips, nz = micro * rows, n // 2, n // 4
    bf, f32, dma = jnp.bfloat16, jnp.float32, pltpu.SemaphoreType.DMA
    vmem = pl.BlockSpec(memory_space=pltpu.VMEM)
    hbm = pl.BlockSpec(memory_space=pltpu.HBM)
    out = pl.pallas_call(
        functools.partial(kernel, n),
        out_shape=jax.ShapeDtypeStruct((m, width), bf),
        in_specs=[vmem, vmem, hbm, hbm, hbm],
        out_specs=vmem,
        scratch_shapes=[
            pltpu.VMEM((chips, 2, 2 * width, ff), bf),
            pltpu.VMEM((chips, ff, 2 * width), bf),
            pltpu.VMEM((layers, n, m, width), bf),
            pltpu.VMEM((m, 2 * width), bf),
            pltpu.VMEM((2, m, ff), f32),
            pltpu.VMEM((m, 128), f32),
            pltpu.VMEM((m, ff), bf),
            pltpu.VMEM((layers, m, width), bf),
            pltpu.VMEM((layers, chips, m, width), bf),
            pltpu.VMEM((layers, chips, m, width), bf),
            pltpu.VMEM((layers, nz, m, width), bf),
            pltpu.VMEM((layers, nz, m, width), bf),
            pltpu.VMEM((layers, nz - 1, m, width), bf),
            pltpu.VMEM((layers, nz, m, width), bf),
            pltpu.VMEM((chips, m, width), f32),
            dma((chips, 2)),
            dma((chips,)),
            dma((layers,)),
            dma((layers, SPLIT, n)),
            dma((layers,)),
            dma((layers, chips)),
            dma((layers, SPLIT, nz)),
            dma((layers, SPLIT, nz)),
        ],
        compiler_params=pltpu.CompilerParams(
            collective_id=0, has_side_effects=True, vmem_limit_bytes=67_043_328
        ),
    )(stream_in.reshape(m, width), norm_gain, w_gate, w_up, w_down)
    return out.reshape(micro, rows, width)


def body(n, stream_in, norm_gain, w_gate, w_up, w_down):
    aligned = stream_in.shape[2] % 128 == 0 and w_gate.shape[2] % 128 == 0 and n % 4 == 0
    held = w_gate[0].size * 6
    if aligned and n // 4 == 4 and stream_in.shape[0] * stream_in.shape[1] % (16 * SPLIT) == 0 and held < 48 * 2**20:
        return fused(n, stream_in, norm_gain, w_gate, w_up, w_down)
    return plain_body(stream_in, norm_gain, w_gate, w_up, w_down)


def solution(mesh):
    return jax.shard_map(
        functools.partial(body, mesh.shape["width"]),
        mesh=mesh,
        in_specs=(
            P(None, "groups", "width"),
            P(),
            P(None, None, "width"),
            P(None, None, "width"),
            P(None, "width", None),
        ),
        out_specs=P(None, "groups", "width"),
        check_vma=False,
    )
```

```python
import functools

import jax
import jax.numpy as jnp
from jax import lax
from jax.experimental import pallas as pl
from jax.experimental.pallas import tpu as pltpu
from jax.sharding import PartitionSpec as P

MESH = pl.DeviceIdType.MESH


def plain_body(stream_in, norm_gain, w_gate, w_up, w_down):
    micro, rows, own_width = stream_in.shape
    stream = stream_in.reshape(micro * rows, own_width)
    for depth in range(w_gate.shape[0]):
        whole = lax.all_gather(stream, "width", axis=1, tiled=True).astype(jnp.float32)
        meansq = jnp.mean(whole * whole, axis=1, keepdims=True)
        normed = (whole * lax.rsqrt(meansq + 1e-05) * norm_gain[depth]).astype(jnp.bfloat16)
        gate_out = jnp.dot(normed, w_gate[depth], preferred_element_type=jnp.float32)
        up_out = jnp.dot(normed, w_up[depth], preferred_element_type=jnp.float32)
        hidden = (jax.nn.silu(gate_out) * up_out).astype(jnp.bfloat16)
        partials = jnp.dot(hidden, w_down[depth], preferred_element_type=jnp.float32)
        branch = lax.psum_scatter(partials, "width", scatter_dimension=1, tiled=True)
        stream = (stream.astype(jnp.float32) + branch).astype(jnp.bfloat16)
    return stream.reshape(micro, rows, own_width)


SPLIT = 2


def kernel(
    n, x_ref, gain_ref, wg_ref, wu_ref, wd_ref, out_ref,
    pair_w, down_w, parts, scaled, acc, squares, hidden, own,
    core_out, core_in, y_out, y_in, z_out, z_in, keep,
    pair_sem, down_sem, gather_send, gather_recv, sum_send, core_recv, y_recv, z_recv,
):
    layers = wg_ref.shape[0]
    m, width = x_ref.shape
    rows = m // SPLIT
    chips, nz = n // 2, n // 4
    chunk = 2 * width
    me = lax.axis_index("width")
    c, y, z = lax.rem(me, 2), lax.rem(me // 2, 2), me // 4

    def device(zi, yi, ci):
        return (zi * 2 + yi) * 2 + ci

    low = z < nz // 2
    inner = (z == 1) | (z == nz - 2)
    mate = z + 1 - 2 * lax.rem(z, 2)
    cross, beyond = jnp.where(low, nz - 2, 1), jnp.where(low, nz - 1, 0)
    core_peer, y_peer = device(z, y, 1 - c), device(z, 1 - y, c)
    near_order = [z, mate, cross, beyond]
    sum_order = [jnp.where(inner, a, b) for a, b in zip([mate, beyond, cross, z], [beyond, cross, mate, z])]

    def pick(i, values):
        value = values[0]
        for at in range(1, len(values)):
            value = jnp.where(i == at, values[at], value)
        return value

    def pair_copy(depth, chip, j):
        src = wg_ref if j == 0 else wu_ref
        span = pl.ds(pl.multiple_of(chip * chunk, chunk), chunk)
        return pltpu.make_async_copy(src.at[depth, span, :], pair_w.at[chip, j], pair_sem.at[chip, j])

    def down_copy(depth, chip):
        cols = pl.ds(pl.multiple_of(chip * chunk, chunk), chunk)
        return pltpu.make_async_copy(wd_ref.at[depth, :, cols], down_w.at[chip], down_sem.at[chip])

    def remote(src, dst, send, recv, dev):
        return pltpu.make_async_remote_copy(
            src_ref=src, dst_ref=dst, send_sem=send, recv_sem=recv,
            device_id={"width": dev}, device_id_type=MESH,
        )

    def piece(h):
        return pl.ds(h * rows, rows)

    sequence = [near_order[0] * 2 + y, near_order[1] * 2 + y, near_order[0] * 2 + 1 - y]
    sequence += [near_order[k] * 2 + y for k in range(2, nz)] + [near_order[k] * 2 + 1 - y for k in range(1, nz)]
    sums = [zi * 2 + 1 - y for zi in sum_order] + [zi * 2 + y for zi in sum_order]

    def load_pair(chip):
        pair_copy(0, chip, 0).start()
        pair_copy(0, chip, 1).start()

    load_pair(sequence[0])

    barrier = pltpu.get_barrier_semaphore()
    peers = [core_peer, y_peer] + [device(zi, y, c) for zi in near_order[1:]]
    for peer in peers:
        pl.semaphore_signal(barrier, inc=1, device_id={"width": peer}, device_id_type=MESH)

    pl.semaphore_wait(barrier, len(peers))

    class Layer:
        def __init__(self, depth):
            self.depth = depth
            self.mine = x_ref if depth == 0 else own.at[depth]

        def to_peer(self, h, owner, dev, mine=False):
            dst = self.part(owner, h)
            src = self.mine.at[piece(h)] if mine else dst
            return remote(src, dst, gather_send.at[self.depth], gather_recv.at[self.depth, h, owner], dev)

        def part(self, owner, h):
            return parts.at[self.depth, owner, piece(h)]

        def arrived(self, h, owner):
            self.to_peer(h, owner, core_peer).wait_recv()

        def send_own(self, h):
            self.to_peer(h, me, device(mate, y, c), True).start()
            self.to_peer(h, me, y_peer, True).start()
            self.to_peer(h, me, device(cross, y, c), True).start()
            self.to_peer(h, me, core_peer, True).start()
            parts[self.depth, me, piece(h)] = self.mine[piece(h)]

        def clear(self):
            acc[...] = jnp.zeros_like(acc)
            squares[...] = jnp.zeros_like(squares)

        def pass_z(self, h, k):
            owner = device(near_order[k], y, c)
            self.arrived(h, owner)
            if k > 1:
                @pl.when(inner)
                def _():
                    self.to_peer(h, owner, device(mate, y, c)).start()
            if h == 0 or k == 1:
                self.to_peer(h, owner, y_peer).start()
            elif k == 2:
                @pl.when(jnp.logical_not(inner))
                def _():
                    self.to_peer(h, owner, y_peer).start()
            self.to_peer(h, owner, core_peer).start()

        def pass_y(self, h, k):
            owner = device(near_order[k], 1 - y, c)
            self.arrived(h, owner)
            if h == 1 and k != 2:
                @pl.when(inner)
                def _():
                    self.to_peer(h, owner, device(mate if k == 3 else cross, y, c)).start()
            self.to_peer(h, owner, core_peer).start()

        def gate_up(self, i):
            depth = self.depth
            chip = pick(i, sequence)
            for h in range(SPLIT):
                self.arrived(h, chip * 2 + 1 - c)
            for h in range(2):
                block = parts[depth, chip * 2 + h].astype(jnp.float32)
                cols = pl.ds(pl.multiple_of((chip * 2 + h) * width, width), width)
                scaled[:, h * width:(h + 1) * width] = (block * gain_ref[depth:depth + 1, cols]).astype(jnp.bfloat16)
                sq = block * block
                total = sq[:, :128]
                for j in range(1, width // 128):
                    total = total + sq[:, j * 128:(j + 1) * 128]
                squares[...] += total
            for j in range(2):
                pair_copy(depth, chip, j).wait()
            for j in range(2):
                acc[j] += jnp.dot(scaled[...], pair_w[chip, j], preferred_element_type=jnp.float32)
            if depth + 1 < layers:
                for j in range(2):
                    pair_copy(depth + 1, chip, j).start()

        def make_hidden(self):
            meansq = jnp.sum(squares[...], axis=1, keepdims=True) / (n * width)
            scale = lax.rsqrt(meansq + 1e-05)
            gate_out = acc[0] * scale
            hidden[...] = (gate_out / (1.0 + jnp.exp(-gate_out)) * (acc[1] * scale)).astype(jnp.bfloat16)

        def core_copy(self, chip):
            return remote(core_out.at[self.depth, chip], core_in.at[self.depth, chip],
                          sum_send.at[self.depth], core_recv.at[self.depth, chip], core_peer)

        def y_copy(self, h, zi):
            return remote(y_out.at[self.depth, zi, piece(h)], y_in.at[self.depth, zi, piece(h)],
                          sum_send.at[self.depth], y_recv.at[self.depth, h, zi], y_peer)

        def z_copy(self, h, t, slot, zi):
            return remote(z_out.at[self.depth, t, piece(h)], z_in.at[self.depth, slot, piece(h)],
                          sum_send.at[self.depth], z_recv.at[self.depth, h, slot], device(zi, y, c))

        def down(self, t):
            chip = pick(t, sums)
            down_copy(self.depth, chip).wait()
            both = jnp.dot(hidden[...], down_w[chip], preferred_element_type=jnp.float32)
            left, right = both[:, :width], both[:, width:]
            core_out[self.depth, chip] = jnp.where(c == 0, right, left).astype(jnp.bfloat16)
            self.core_copy(chip).start()
            keep[chip] = jnp.where(c == 0, left, right)
            if self.depth + 1 < layers:
                down_copy(self.depth + 1, chip).start()

        def core_sum(self, h, chip):
            return keep[chip, piece(h)] + core_in[self.depth, chip, piece(h)].astype(jnp.float32)

        def far(self, h, t):
            zi, chip = sum_order[t], sums[t]
            if h == 0:
                self.core_copy(chip).wait_recv()
            y_out[self.depth, zi, piece(h)] = self.core_sum(h, chip).astype(jnp.bfloat16)
            self.y_copy(h, zi).start()

        def near_sum(self, h, t):
            zi, chip = sum_order[t], sums[nz + t]
            if h == 0:
                self.core_copy(chip).wait_recv()
            self.y_copy(h, zi).wait_recv()
            return self.core_sum(h, chip) + y_in[self.depth, zi, piece(h)].astype(jnp.float32)

        def near(self, h, t):
            total = self.near_sum(h, t)
            if t == 0:
                z_out[self.depth, t, piece(h)] = total.astype(jnp.bfloat16)
            else:
                @pl.when(inner)
                def _():
                    self.z_copy(h, t, t - 1, mate).wait_recv()
                    met = z_in[self.depth, t - 1, piece(h)].astype(jnp.float32)
                    z_out[self.depth, t, piece(h)] = (total + met).astype(jnp.bfloat16)

                @pl.when(jnp.logical_not(inner))
                def _():
                    z_out[self.depth, t, piece(h)] = total.astype(jnp.bfloat16)
            slot = jnp.where(inner, 2 if t == 0 else 3, t)
            self.z_copy(h, t, slot, jnp.where(inner, sum_order[t], mate)).start()

        def final(self, h):
            total = self.near_sum(h, nz - 1) + self.mine[piece(h)].astype(jnp.float32)
            for slot in (2, 3):
                self.z_copy(h, 0, slot, mate).wait_recv()
                total = total + z_in[self.depth, slot, piece(h)].astype(jnp.float32)
            if self.depth + 1 < layers:
                own[self.depth + 1, piece(h)] = total.astype(jnp.bfloat16)
                Layer(self.depth + 1).send_own(h)
            else:
                out_ref[piece(h)] = total.astype(jnp.bfloat16)

        def sent(self):
            whole = parts.at[self.depth, pl.ds(0, n - 3)]
            pltpu.make_async_copy(whole, whole, gather_send.at[self.depth]).wait()
            one = self.part(0, 0)
            pltpu.make_async_copy(one, one, gather_send.at[self.depth]).wait()

            @pl.when(inner)
            def _():
                three = parts.at[self.depth, pl.ds(0, nz - 1)]
                pltpu.make_async_copy(three, three, gather_send.at[self.depth]).wait()

            whole = parts.at[self.depth, pl.ds(0, n - 1)]
            pltpu.make_async_copy(whole, whole, sum_send.at[self.depth]).wait()

    def steps(count, tasks, body):
        @pl.loop(0, count)
        def _(i):
            for at in sorted(set(at for at, _ in tasks)):
                @pl.when(i == at)
                def _():
                    for where, task in tasks:
                        if where == at:
                            task()
            body(i)

    def call(method, *args):
        return lambda: method(*args)

    every = [Layer(depth) for depth in range(layers)]
    for depth, layer in enumerate(every):
        if depth == 0:
            for h in range(SPLIT):
                layer.send_own(h)
            for chip in sequence[1:]:
                load_pair(chip)
            for chip in sums:
                down_copy(0, chip).start()
        layer.clear()
        tasks = []
        H = range(SPLIT)
        tasks += [(1, call(layer.pass_z, h, 1)) for h in H] + [(1, call(layer.pass_y, h, 0)) for h in H]
        tasks += [(2, call(layer.pass_z, h, 2)) for h in H]
        tasks += [(3, call(layer.pass_z, h, 3)) for h in H]
        tasks += [(k + 3, call(layer.pass_y, h, k)) for k in range(1, nz) for h in H]
        steps(chips, tasks, layer.gate_up)
        layer.make_hidden()
        tasks = []
        tasks += [(t + 2, call(layer.far, h, t)) for t in range(nz) for h in range(SPLIT)]
        steps(chips, tasks, layer.down)
        before = layer
        for t in range(nz - 1):
            for h in range(SPLIT):
                layer.near(h, t)
        for h in range(SPLIT):
            layer.final(h)
    for layer in every:
        layer.sent()


def fused(n, stream_in, norm_gain, w_gate, w_up, w_down):
    micro, rows, width = stream_in.shape
    layers, d, ff = w_gate.shape
    m, chips, nz = micro * rows, n // 2, n // 4
    bf, f32, dma = jnp.bfloat16, jnp.float32, pltpu.SemaphoreType.DMA
    vmem = pl.BlockSpec(memory_space=pltpu.VMEM)
    hbm = pl.BlockSpec(memory_space=pltpu.HBM)
    out = pl.pallas_call(
        functools.partial(kernel, n),
        out_shape=jax.ShapeDtypeStruct((m, width), bf),
        in_specs=[vmem, vmem, hbm, hbm, hbm],
        out_specs=vmem,
        scratch_shapes=[
            pltpu.VMEM((chips, 2, 2 * width, ff), bf),
            pltpu.VMEM((chips, ff, 2 * width), bf),
            pltpu.VMEM((layers, n, m, width), bf),
            pltpu.VMEM((m, 2 * width), bf),
            pltpu.VMEM((2, m, ff), f32),
            pltpu.VMEM((m, 128), f32),
            pltpu.VMEM((m, ff), bf),
            pltpu.VMEM((layers, m, width), bf),
            pltpu.VMEM((layers, chips, m, width), bf),
            pltpu.VMEM((layers, chips, m, width), bf),
            pltpu.VMEM((layers, nz, m, width), bf),
            pltpu.VMEM((layers, nz, m, width), bf),
            pltpu.VMEM((layers, nz - 1, m, width), bf),
            pltpu.VMEM((layers, nz, m, width), bf),
            pltpu.VMEM((chips, m, width), f32),
            dma((chips, 2)),
            dma((chips,)),
            dma((layers,)),
            dma((layers, SPLIT, n)),
            dma((layers,)),
            dma((layers, chips)),
            dma((layers, SPLIT, nz)),
            dma((layers, SPLIT, nz)),
        ],
        compiler_params=pltpu.CompilerParams(
            collective_id=0, has_side_effects=True, vmem_limit_bytes=67_043_328
        ),
    )(stream_in.reshape(m, width), norm_gain, w_gate, w_up, w_down)
    return out.reshape(micro, rows, width)


def body(n, stream_in, norm_gain, w_gate, w_up, w_down):
    aligned = stream_in.shape[2] % 128 == 0 and w_gate.shape[2] % 128 == 0 and n % 4 == 0
    held = w_gate[0].size * 6
    if aligned and n // 4 == 4 and stream_in.shape[0] * stream_in.shape[1] % (16 * SPLIT) == 0 and held < 48 * 2**20:
        return fused(n, stream_in, norm_gain, w_gate, w_up, w_down)
    return plain_body(stream_in, norm_gain, w_gate, w_up, w_down)


def solution(mesh):
    return jax.shard_map(
        functools.partial(body, mesh.shape["width"]),
        mesh=mesh,
        in_specs=(
            P(None, "groups", "width"),
            P(),
            P(None, None, "width"),
            P(None, None, "width"),
            P(None, "width", None),
        ),
        out_specs=P(None, "groups", "width"),
        check_vma=False,
    )
```

```python
import functools

import jax
import jax.numpy as jnp
from jax import lax
from jax.experimental import pallas as pl
from jax.experimental.pallas import tpu as pltpu
from jax.sharding import PartitionSpec as P

MESH = pl.DeviceIdType.MESH


def plain_body(stream_in, norm_gain, w_gate, w_up, w_down):
    micro, rows, own_width = stream_in.shape
    stream = stream_in.reshape(micro * rows, own_width)
    for depth in range(w_gate.shape[0]):
        whole = lax.all_gather(stream, "width", axis=1, tiled=True).astype(jnp.float32)
        meansq = jnp.mean(whole * whole, axis=1, keepdims=True)
        normed = (whole * lax.rsqrt(meansq + 1e-05) * norm_gain[depth]).astype(jnp.bfloat16)
        gate_out = jnp.dot(normed, w_gate[depth], preferred_element_type=jnp.float32)
        up_out = jnp.dot(normed, w_up[depth], preferred_element_type=jnp.float32)
        hidden = (jax.nn.silu(gate_out) * up_out).astype(jnp.bfloat16)
        partials = jnp.dot(hidden, w_down[depth], preferred_element_type=jnp.float32)
        branch = lax.psum_scatter(partials, "width", scatter_dimension=1, tiled=True)
        stream = (stream.astype(jnp.float32) + branch).astype(jnp.bfloat16)
    return stream.reshape(micro, rows, own_width)


SPLIT = 2


def kernel(
    n, x_ref, gain_ref, wg_ref, wu_ref, wd_ref, out_ref,
    pair_w, down_w, parts, scaled, acc, squares, hidden, own,
    core_out, core_in, y_out, y_in, z_out, z_in, keep,
    pair_sem, down_sem, gather_send, gather_recv, sum_send, core_recv, y_recv, z_recv,
):
    layers = wg_ref.shape[0]
    m, width = x_ref.shape
    rows = m // SPLIT
    chips, nz = n // 2, n // 4
    chunk = 2 * width
    me = lax.axis_index("width")
    c, y, z = lax.rem(me, 2), lax.rem(me // 2, 2), me // 4

    def device(zi, yi, ci):
        return (zi * 2 + yi) * 2 + ci

    low = z < nz // 2
    inner = (z == 1) | (z == nz - 2)
    mate = z + 1 - 2 * lax.rem(z, 2)
    cross, beyond = jnp.where(low, nz - 2, 1), jnp.where(low, nz - 1, 0)
    core_peer, y_peer = device(z, y, 1 - c), device(z, 1 - y, c)
    near_order = [z, mate, cross, beyond]
    sum_order = [jnp.where(inner, a, b) for a, b in zip([mate, beyond, cross, z], [beyond, cross, mate, z])]

    def pick(i, values):
        value = values[0]
        for at in range(1, len(values)):
            value = jnp.where(i == at, values[at], value)
        return value

    def pair_copy(depth, chip, j):
        src = wg_ref if j == 0 else wu_ref
        span = pl.ds(pl.multiple_of(chip * chunk, chunk), chunk)
        return pltpu.make_async_copy(src.at[depth, span, :], pair_w.at[chip, j], pair_sem.at[chip, j])

    def down_copy(depth, chip):
        cols = pl.ds(pl.multiple_of(chip * chunk, chunk), chunk)
        return pltpu.make_async_copy(wd_ref.at[depth, :, cols], down_w.at[chip], down_sem.at[chip])

    def remote(src, dst, send, recv, dev):
        return pltpu.make_async_remote_copy(
            src_ref=src, dst_ref=dst, send_sem=send, recv_sem=recv,
            device_id={"width": dev}, device_id_type=MESH,
        )

    def piece(h):
        return pl.ds(h * rows, rows)

    sequence = [near_order[0] * 2 + y, near_order[1] * 2 + y, near_order[0] * 2 + 1 - y]
    sequence += [near_order[k] * 2 + y for k in range(2, nz)] + [near_order[k] * 2 + 1 - y for k in range(1, nz)]
    sums = [zi * 2 + 1 - y for zi in sum_order] + [zi * 2 + y for zi in sum_order]

    def load_pair(chip):
        pair_copy(0, chip, 0).start()
        pair_copy(0, chip, 1).start()

    load_pair(sequence[0])

    barrier = pltpu.get_barrier_semaphore()
    peers = [core_peer, y_peer] + [device(zi, y, c) for zi in near_order[1:]]
    for peer in peers:
        pl.semaphore_signal(barrier, inc=1, device_id={"width": peer}, device_id_type=MESH)

    pl.semaphore_wait(barrier, len(peers))

    class Layer:
        def __init__(self, depth):
            self.depth = depth
            self.mine = x_ref if depth == 0 else own.at[depth]

        def to_peer(self, h, owner, dev, mine=False):
            dst = self.part(owner, h)
            src = self.mine.at[piece(h)] if mine else dst
            return remote(src, dst, gather_send.at[self.depth], gather_recv.at[self.depth, h, owner], dev)

        def part(self, owner, h):
            return parts.at[self.depth, owner, piece(h)]

        def arrived(self, h, owner):
            self.to_peer(h, owner, core_peer).wait_recv()

        def send_own(self, h):
            self.to_peer(h, me, y_peer, True).start()
            self.to_peer(h, me, device(mate, y, c), True).start()
            self.to_peer(h, me, device(cross, y, c), True).start()
            self.to_peer(h, me, core_peer, True).start()
            parts[self.depth, me, piece(h)] = self.mine[piece(h)]

        def clear(self):
            acc[...] = jnp.zeros_like(acc)
            squares[...] = jnp.zeros_like(squares)

        def pass_z(self, h, k):
            owner = device(near_order[k], y, c)
            self.arrived(h, owner)
            if k > 1:
                @pl.when(inner)
                def _():
                    self.to_peer(h, owner, device(mate, y, c)).start()
            if h == 0 or k == 1:
                self.to_peer(h, owner, y_peer).start()
            elif k == 2:
                @pl.when(jnp.logical_not(inner))
                def _():
                    self.to_peer(h, owner, y_peer).start()
            self.to_peer(h, owner, core_peer).start()

        def pass_y(self, h, k):
            owner = device(near_order[k], 1 - y, c)
            self.arrived(h, owner)
            if h == 1 and k != 2:
                @pl.when(inner)
                def _():
                    self.to_peer(h, owner, device(mate if k == 3 else cross, y, c)).start()
            self.to_peer(h, owner, core_peer).start()

        def gate_up(self, i):
            depth = self.depth
            chip = pick(i, sequence)
            for h in range(SPLIT):
                self.arrived(h, chip * 2 + 1 - c)
            for h in range(2):
                block = parts[depth, chip * 2 + h].astype(jnp.float32)
                cols = pl.ds(pl.multiple_of((chip * 2 + h) * width, width), width)
                scaled[:, h * width:(h + 1) * width] = (block * gain_ref[depth:depth + 1, cols]).astype(jnp.bfloat16)
                sq = block * block
                total = sq[:, :128]
                for j in range(1, width // 128):
                    total = total + sq[:, j * 128:(j + 1) * 128]
                squares[...] += total
            for j in range(2):
                pair_copy(depth, chip, j).wait()
            for j in range(2):
                acc[j] += jnp.dot(scaled[...], pair_w[chip, j], preferred_element_type=jnp.float32)
            if depth + 1 < layers:
                for j in range(2):
                    pair_copy(depth + 1, chip, j).start()

        def make_hidden(self):
            meansq = jnp.sum(squares[...], axis=1, keepdims=True) / (n * width)
            scale = lax.rsqrt(meansq + 1e-05)
            gate_out = acc[0] * scale
            hidden[...] = (gate_out / (1.0 + jnp.exp(-gate_out)) * (acc[1] * scale)).astype(jnp.bfloat16)

        def core_copy(self, chip):
            return remote(core_out.at[self.depth, chip], core_in.at[self.depth, chip],
                          sum_send.at[self.depth], core_recv.at[self.depth, chip], core_peer)

        def y_copy(self, h, zi):
            return remote(y_out.at[self.depth, zi, piece(h)], y_in.at[self.depth, zi, piece(h)],
                          sum_send.at[self.depth], y_recv.at[self.depth, h, zi], y_peer)

        def z_copy(self, h, t, slot, zi):
            return remote(z_out.at[self.depth, t, piece(h)], z_in.at[self.depth, slot, piece(h)],
                          sum_send.at[self.depth], z_recv.at[self.depth, h, slot], device(zi, y, c))

        def down(self, t):
            chip = pick(t, sums)
            down_copy(self.depth, chip).wait()
            both = jnp.dot(hidden[...], down_w[chip], preferred_element_type=jnp.float32)
            left, right = both[:, :width], both[:, width:]
            core_out[self.depth, chip] = jnp.where(c == 0, right, left).astype(jnp.bfloat16)
            self.core_copy(chip).start()
            keep[chip] = jnp.where(c == 0, left, right)
            if self.depth + 1 < layers:
                down_copy(self.depth + 1, chip).start()

        def core_sum(self, h, chip):
            return keep[chip, piece(h)] + core_in[self.depth, chip, piece(h)].astype(jnp.float32)

        def far(self, h, t):
            zi, chip = sum_order[t], sums[t]
            if h == 0:
                self.core_copy(chip).wait_recv()
            y_out[self.depth, zi, piece(h)] = self.core_sum(h, chip).astype(jnp.bfloat16)
            self.y_copy(h, zi).start()

        def near_sum(self, h, t):
            zi, chip = sum_order[t], sums[nz + t]
            if h == 0:
                self.core_copy(chip).wait_recv()
            self.y_copy(h, zi).wait_recv()
            return self.core_sum(h, chip) + y_in[self.depth, zi, piece(h)].astype(jnp.float32)

        def near(self, h, t):
            total = self.near_sum(h, t)
            if t == 0:
                z_out[self.depth, t, piece(h)] = total.astype(jnp.bfloat16)
            else:
                @pl.when(inner)
                def _():
                    self.z_copy(h, t, t - 1, mate).wait_recv()
                    met = z_in[self.depth, t - 1, piece(h)].astype(jnp.float32)
                    z_out[self.depth, t, piece(h)] = (total + met).astype(jnp.bfloat16)

                @pl.when(jnp.logical_not(inner))
                def _():
                    z_out[self.depth, t, piece(h)] = total.astype(jnp.bfloat16)
            slot = jnp.where(inner, 2 if t == 0 else 3, t)
            self.z_copy(h, t, slot, jnp.where(inner, sum_order[t], mate)).start()

        def final(self, h):
            total = self.near_sum(h, nz - 1) + self.mine[piece(h)].astype(jnp.float32)
            for slot in (2, 3):
                self.z_copy(h, 0, slot, mate).wait_recv()
                total = total + z_in[self.depth, slot, piece(h)].astype(jnp.float32)
            if self.depth + 1 < layers:
                own[self.depth + 1, piece(h)] = total.astype(jnp.bfloat16)
                Layer(self.depth + 1).send_own(h)
            else:
                out_ref[piece(h)] = total.astype(jnp.bfloat16)

        def sent(self):
            whole = parts.at[self.depth, pl.ds(0, n - 3)]
            pltpu.make_async_copy(whole, whole, gather_send.at[self.depth]).wait()
            one = self.part(0, 0)
            pltpu.make_async_copy(one, one, gather_send.at[self.depth]).wait()

            @pl.when(inner)
            def _():
                three = parts.at[self.depth, pl.ds(0, nz - 1)]
                pltpu.make_async_copy(three, three, gather_send.at[self.depth]).wait()

            whole = parts.at[self.depth, pl.ds(0, n - 1)]
            pltpu.make_async_copy(whole, whole, sum_send.at[self.depth]).wait()

    def steps(count, tasks, body):
        @pl.loop(0, count)
        def _(i):
            for at in sorted(set(at for at, _ in tasks)):
                @pl.when(i == at)
                def _():
                    for where, task in tasks:
                        if where == at:
                            task()
            body(i)

    def call(method, *args):
        return lambda: method(*args)

    every = [Layer(depth) for depth in range(layers)]
    for depth, layer in enumerate(every):
        if depth == 0:
            for h in range(SPLIT):
                layer.send_own(h)
            for chip in sequence[1:]:
                load_pair(chip)
            for chip in sums:
                down_copy(0, chip).start()
        layer.clear()
        tasks = []
        H = range(SPLIT)
        tasks += [(1, call(layer.pass_z, h, 1)) for h in H] + [(1, call(layer.pass_y, h, 0)) for h in H]
        tasks += [(2, call(layer.pass_z, h, 2)) for h in H]
        tasks += [(3, call(layer.pass_z, h, 3)) for h in H]
        tasks += [(k + 3, call(layer.pass_y, h, k)) for k in range(1, nz) for h in H]
        steps(chips, tasks, layer.gate_up)
        layer.make_hidden()
        tasks = []
        tasks += [(t + 2, call(layer.far, h, t)) for t in range(nz) for h in range(SPLIT)]
        steps(chips, tasks, layer.down)
        before = layer
        for t in range(nz - 1):
            for h in range(SPLIT):
                layer.near(h, t)
        for h in range(SPLIT):
            layer.final(h)
    for layer in every:
        layer.sent()


def fused(n, stream_in, norm_gain, w_gate, w_up, w_down):
    micro, rows, width = stream_in.shape
    layers, d, ff = w_gate.shape
    m, chips, nz = micro * rows, n // 2, n // 4
    bf, f32, dma = jnp.bfloat16, jnp.float32, pltpu.SemaphoreType.DMA
    vmem = pl.BlockSpec(memory_space=pltpu.VMEM)
    hbm = pl.BlockSpec(memory_space=pltpu.HBM)
    out = pl.pallas_call(
        functools.partial(kernel, n),
        out_shape=jax.ShapeDtypeStruct((m, width), bf),
        in_specs=[vmem, vmem, hbm, hbm, hbm],
        out_specs=vmem,
        scratch_shapes=[
            pltpu.VMEM((chips, 2, 2 * width, ff), bf),
            pltpu.VMEM((chips, ff, 2 * width), bf),
            pltpu.VMEM((layers, n, m, width), bf),
            pltpu.VMEM((m, 2 * width), bf),
            pltpu.VMEM((2, m, ff), f32),
            pltpu.VMEM((m, 128), f32),
            pltpu.VMEM((m, ff), bf),
            pltpu.VMEM((layers, m, width), bf),
            pltpu.VMEM((layers, chips, m, width), bf),
            pltpu.VMEM((layers, chips, m, width), bf),
            pltpu.VMEM((layers, nz, m, width), bf),
            pltpu.VMEM((layers, nz, m, width), bf),
            pltpu.VMEM((layers, nz - 1, m, width), bf),
            pltpu.VMEM((layers, nz, m, width), bf),
            pltpu.VMEM((chips, m, width), f32),
            dma((chips, 2)),
            dma((chips,)),
            dma((layers,)),
            dma((layers, SPLIT, n)),
            dma((layers,)),
            dma((layers, chips)),
            dma((layers, SPLIT, nz)),
            dma((layers, SPLIT, nz)),
        ],
        compiler_params=pltpu.CompilerParams(
            collective_id=0, has_side_effects=True, vmem_limit_bytes=67_043_328
        ),
    )(stream_in.reshape(m, width), norm_gain, w_gate, w_up, w_down)
    return out.reshape(micro, rows, width)


def body(n, stream_in, norm_gain, w_gate, w_up, w_down):
    aligned = stream_in.shape[2] % 128 == 0 and w_gate.shape[2] % 128 == 0 and n % 4 == 0
    held = w_gate[0].size * 6
    if aligned and n // 4 == 4 and stream_in.shape[0] * stream_in.shape[1] % (16 * SPLIT) == 0 and held < 48 * 2**20:
        return fused(n, stream_in, norm_gain, w_gate, w_up, w_down)
    return plain_body(stream_in, norm_gain, w_gate, w_up, w_down)


def solution(mesh):
    return jax.shard_map(
        functools.partial(body, mesh.shape["width"]),
        mesh=mesh,
        in_specs=(
            P(None, "groups", "width"),
            P(),
            P(None, None, "width"),
            P(None, None, "width"),
            P(None, "width", None),
        ),
        out_specs=P(None, "groups", "width"),
        check_vma=False,
    )
```
